256 devices in a mesh: ctx: 64 (over y, z_lo, x, core), tp: 4 (over z_hi).
Axes of the slice: x: 4, y: 4, z: 8 (z_hi: 4, z_lo: 2; z = z_hi * 2 + z_lo), core: 2. Of those that a mesh axis runs over, the one named last changes fastest.
Arguments:
- queries: bfloat16 [16384, 2048], P('ctx', 'tp'), may hold values from -8 to 8
- span_keys: bfloat16 [16384, 1024], P('ctx', 'tp'), may hold values from -6 to 6
- span_values: bfloat16 [16384, 1024], P('ctx', 'tp'), may hold values from -6 to 6
- cache_keys: bfloat16 [8192, 1024], P('ctx', 'tp'), may hold values from -8 to 8
- cache_values: bfloat16 [8192, 1024], P('ctx', 'tp'), may hold values from -6 to 6
- out_weight: bfloat16 [2048, 3840], P('tp'), may hold values from -0.125 to 0.125
- offsets: int32 [64], replicated, may hold values from 0 to 16128, as said below
- earlier_block_slot: int32 [128], replicated, may hold values from 0 to 127, each once
- prior_block_count: int32 [1], replicated, may hold values from 32 to 127
Outputs:
- projected: bfloat16 [16384, 3840], P('ctx', 'tp')
The draws below stay inside these ranges and needn't reach their ends.
Inputs may be any that keep to these rules, and one draw needn't show every extreme that they name: `offsets`: a permutation of the multiples of 256 below 16384. Block b of the earlier prompt lies in slot earlier_block_slot[b]; slot s is held by index s // 2 of ctx; only blocks below prior_block_count[0] are valid.
All inputs are finite; a program needn't handle non-finite values.
Results may differ from the reference program's by a relative error of at most 0.012.
Values may be sent and summed in bfloat16 or wider, within the bound.
No kernel may reach another device: no remote copies, remote signals or barrier semaphores. Data moves between devices by JAX's collectives and lax.ppermute only.
A program may use at most 192 MiB of HBM per device.

```python
import math
import jax
import jax.numpy as jnp
from jax import lax

D = 3840
E = 256
Q_HEADS = 8
KV_HEADS = 4
T_DEV = 256
BLK = 64
SHARDS = 64
TOKENS = 16384
TOTAL_SLOTS = 128
CACHE_ROWS = 8192


def draw_queries(key, part):
    shape_all = (TOKENS, Q_HEADS * E)
    return (2.7 * jax.random.truncated_normal(key, -2.9, 2.9, shape_all, jnp.float32)).astype(jnp.bfloat16)


def draw_cache_keys(key, part):
    shape_all = (CACHE_ROWS, KV_HEADS * E)
    return jax.random.truncated_normal(jax.random.fold_in(key, 19), -6.0, 6.0, shape_all, jnp.float32).astype(jnp.bfloat16)


def draw_offsets(key, part):
    return jax.random.permutation(key, jnp.arange(SHARDS, dtype=jnp.int32)) * T_DEV


def steps_of(own_key, shape, split, smallest, high):
    def one(position, shards_of):
        heights = jax.random.uniform(jax.random.fold_in(jax.random.fold_in(own_key, 6), position), (shards_of,), jnp.float32, smallest / len(split), high / len(split))
        return jnp.repeat(jnp.exp(heights), shape[position] // shards_of).reshape((-1,) + (1,) * (len(shape) - position - 1))

    loudness = one(*split[0])
    for cut in split[1:]:
        loudness = loudness * one(*cut)
    return loudness


def noise(rng, extent, deviation, most, cuts=(), held_as=jnp.bfloat16):
    array = deviation * jax.random.normal(rng, extent, jnp.float32)
    if cuts:
        array = array * steps_of(rng, extent, cuts, -0.22, 0.18)
    return jnp.clip(array, -most, most).astype(held_as)


def setup_inputs(seed: int = 0) -> dict:
    key_of = jax.random.split(jax.random.key(seed), 10)
    return {
        "queries": draw_queries(jax.random.fold_in(key_of[9], 71), 0),
        "span_keys": noise(key_of[1], (TOKENS, KV_HEADS * E), 1.0, 6.0, ((0, 64), (1, 4))),
        "span_values": noise(key_of[2], (TOKENS, KV_HEADS * E), 1.0, 6.0, ((0, 64), (1, 4))),
        "cache_keys": draw_cache_keys(jax.random.fold_in(key_of[9], 71), 0),
        "cache_values": noise(key_of[4], (CACHE_ROWS, KV_HEADS * E), 1.0, 6.0, ((0, 64), (1, 4))),
        "out_weight": noise(key_of[5], (Q_HEADS * E, D), (Q_HEADS * E) ** -0.5, 0.125, ((0, 4),)),
        "offsets": draw_offsets(jax.random.fold_in(key_of[9], 71), 0),
        "earlier_block_slot": jax.random.permutation(key_of[7], TOTAL_SLOTS).astype(jnp.int32),
        "prior_block_count": jax.random.randint(key_of[8], (1,), TOTAL_SLOTS // 4, TOTAL_SLOTS).astype(jnp.int32),
    }


def reference(queries, span_keys, span_values, cache_keys, cache_values, out_weight, offsets, earlier_block_slot, prior_block_count):
    count_tokens = queries.shape[0]
    row_index = jnp.arange(count_tokens, dtype=jnp.int32)
    positions = offsets[row_index // T_DEV] + row_index % T_DEV
    slot_count = earlier_block_slot.shape[0]
    slot_owner_block = jnp.zeros((slot_count,), jnp.int32).at[earlier_block_slot].set(jnp.arange(slot_count, dtype=jnp.int32))
    cache_in_use = jnp.repeat(slot_owner_block < prior_block_count[0], BLK)
    all_keys = jnp.concatenate([cache_keys, span_keys], axis=0)
    all_values = jnp.concatenate([cache_values, span_values], axis=0)
    query_group_width = Q_HEADS // KV_HEADS
    scale = E ** -0.5
    block_rows = math.gcd(count_tokens, 256)

    def one_block(block_index):
        start = (block_index * block_rows).astype(jnp.int32)
        query_block = lax.dynamic_slice_in_dim(queries, start, block_rows, 0)
        query_pos = lax.dynamic_slice_in_dim(positions, start, block_rows, 0)
        allowed = jnp.concatenate([jnp.broadcast_to(cache_in_use[None, :], (block_rows, cache_in_use.shape[0])), positions[None, :] <= query_pos[:, None]], axis=1)
        results = []
        for head_index in range(Q_HEADS):
            kv_index = head_index // query_group_width
            query_head = query_block[:, head_index * E:(head_index + 1) * E]
            key_head = all_keys[:, kv_index * E:(kv_index + 1) * E]
            value_head = all_values[:, kv_index * E:(kv_index + 1) * E]
            scores = jnp.dot(query_head, key_head.T, preferred_element_type=jnp.float32) * scale
            scores = jnp.where(allowed, scores, -1e30)
            largest = jnp.max(scores, axis=1, keepdims=True)
            weights = jnp.where(allowed, jnp.exp(scores - largest), 0.0)
            total = jnp.sum(weights, axis=1, keepdims=True)
            summed = jnp.dot(weights.astype(jnp.bfloat16), value_head, preferred_element_type=jnp.float32)
            results.append(summed / total)
        return jnp.concatenate(results, axis=1).astype(jnp.bfloat16)

    attended = lax.map(one_block, jnp.arange(count_tokens // block_rows, dtype=jnp.int32))
    attended = attended.reshape(count_tokens, Q_HEADS * E)
    return jnp.dot(attended, out_weight, preferred_element_type=jnp.float32).astype(jnp.bfloat16)
```

```python
import functools

import numpy as np
import jax
import jax.numpy as jnp
from jax import lax
from jax.experimental import pallas as pl
from jax.experimental.pallas import tpu as pltpu
from jax.sharding import PartitionSpec as P

E = 256
BLK = 64
T = 256
CB = 128
DR = 2 * T + 2 * CB
NY, NZ, NX, NC = 4, 2, 4, 2
C = np.float32(1.4426950408889634 / 16.0)
LOW = -1e30
OUT = -2e30
TK = 1024
SUB = 256
ST = 16


def _ctx(y, z, x, c):
    return (((y % NY) * NZ + z % NZ) * NX + x % NX) * NC + c % NC


def _perm(step):
    dy, dz, dx, dc = step
    return [
        (_ctx(y, z, x, c), _ctx(y + dy, z + dz, x + dx, c + dc))
        for y in range(NY)
        for z in range(NZ)
        for x in range(NX)
        for c in range(NC)
    ]


def _send(a, dy=0, dz=0, dx=0, dc=0):
    return lax.ppermute(a, "ctx", _perm((dy, dz, dx, dc)))


def _send_tp(a, d):
    return lax.ppermute(a, "tp", [(i, (i + d) % 4) for i in range(4)])


def _flash_body(n, first, last, offs, live, ids, qids, *refs):
    nb = n
    q_in = refs[:4]
    blocks = refs[4 : 4 + nb]
    refs = refs[4 + nb :]
    if not first:
        m_in, l_in, a_in = refs[:3]
        refs = refs[3:]
    if last:
        outs = refs[:4]
        refs = refs[4:]
    else:
        m_out, l_out, a_out = refs[:3]
        refs = refs[3:]
    qb, kb, vb, m_sc, l_sc, a_sc, qsem, ksem, vsem, ssem = refs

    copies = []
    for i in range(4):
        cp = pltpu.make_async_copy(q_in[i], qb.at[i], qsem.at[i])
        cp.start()
        copies.append(cp)
    if not first:
        for i, (src, dst) in enumerate(((m_in, m_sc), (l_in, l_sc), (a_in, a_sc))):
            cp = pltpu.make_async_copy(src, dst, ssem.at[i])
            cp.start()
            copies.append(cp)
    koff = [offs[ids[j]] for j in range(nb)]
    alive = [live[ids[j // 2] * 2 + j % 2] for j in range(2 * nb)]
    n_live = alive[0]
    for a in alive[1:]:
        n_live = n_live + a
    span0 = n_live * BLK
    dead0 = span0 + nb * T
    seen = jnp.int32(0)
    for j in range(nb):
        rank = jnp.int32(0)
        for i in range(nb):
            if i != j:
                rank = rank + (koff[i] < koff[j]).astype(jnp.int32)
        row = pl.multiple_of(span0 + rank * T, BLK)
        for s, (dst, sem) in enumerate(((kb, ksem), (vb, vsem))):
            cp = pltpu.make_async_copy(
                blocks[j].at[pl.ds(s * T, T)], dst.at[pl.ds(row, T)], sem.at[3 * j]
            )
            cp.start()
            copies.append(cp)
        for h in range(2):
            on = alive[2 * j + h]
            row = jnp.where(on > 0, seen * BLK, dead0 + (2 * j + h - seen) * BLK)
            row = pl.multiple_of(row, BLK)
            seen = seen + on
            for s, (dst, sem) in enumerate(((kb, ksem), (vb, vsem))):
                cp = pltpu.make_async_copy(
                    blocks[j].at[pl.ds(2 * T + s * CB + h * BLK, BLK)],
                    dst.at[pl.ds(row, BLK)],
                    sem.at[3 * j + 1 + h],
                )
                cp.start()
                copies.append(cp)
    for cp in copies:
        cp.wait()

    def shard(qi, _):
        qid = qids[qi]
        qoff = offs[qid]
        before = jnp.int32(0)
        own = jnp.int32(0)
        for j in range(nb):
            before = before + (koff[j] < qoff).astype(jnp.int32)
            own = own + (ids[j] == qid).astype(jnp.int32)
        base = span0 + before * T
        total = base + own * T
        rows = pl.ds(pl.multiple_of(qi * 2 * T, 2 * T), 2 * T)
        if first:
            m_sc[rows] = jnp.full((2 * T, 128), LOW, jnp.float32)
            l_sc[rows] = jnp.zeros((2 * T, 128), jnp.float32)
            a_sc[rows] = jnp.zeros((2 * T, E), jnp.float32)

        def tile(start, width, masked):
            at = pl.ds(pl.multiple_of(start, SUB), width)
            ks = kb[at, :]
            vs = vb[at, :]
            for h in range(2):
                hr = pl.ds(pl.multiple_of(qi * 2 * T + h * T, T), T)
                q = qb[qi, :, h * E : (h + 1) * E]
                s = lax.dot_general(
                    q, ks, (((1,), (1,)), ((), ())), preferred_element_type=jnp.float32
                )
                if masked:
                    col = lax.broadcasted_iota(jnp.int32, s.shape, 1)
                    tok = lax.broadcasted_iota(jnp.int32, s.shape, 0)
                    s = jnp.where(col < (base - start) + own * (tok + 1), s, OUT)
                old = m_sc[hr]
                new = jnp.maximum(old, jnp.max(s, axis=1, keepdims=True))
                p = jnp.exp2((s - jnp.tile(new, (1, width // 128))) * C)
                f = jnp.exp2((old - new) * C)
                part = p[:, :128]
                for i in range(1, width // 128):
                    part = part + p[:, i * 128 : (i + 1) * 128]
                l_sc[hr] = l_sc[hr] * f + part
                up = jnp.dot(p.astype(jnp.bfloat16), vs, preferred_element_type=jnp.float32)
                a_sc[hr] = a_sc[hr] * jnp.tile(f, (1, 2)) + up
                m_sc[hr] = new

        full = base // TK

        def step(t, _):
            tile(t * TK, TK, False)
            return 0

        lax.fori_loop(0, full, step, 0)
        rest = pl.cdiv(total - full * TK, SUB)
        wide = TK // SUB

        @pl.when(rest >= wide)
        def _():
            tile(full * TK, TK, True)

        done = full * wide + jnp.where(rest >= wide, wide, 0)
        rest = rest - jnp.where(rest >= wide, wide, 0)
        for w in range(1, wide):

            @pl.when(rest == w)
            def _():
                tile(done * SUB, w * SUB, True)

        if last:
            stats = jnp.zeros((T, 128), jnp.float32)
            lane = lax.broadcasted_iota(jnp.int32, (T, 128), 1)
            for h in range(2):
                hr = pl.ds(pl.multiple_of(qi * 2 * T + h * T, T), T)
                ls = jnp.sum(l_sc[hr], axis=1, keepdims=True)
                some = ls > 0.0
                safe = jnp.where(some, ls, 1.0)
                o = a_sc[hr] * (1.0 / safe)
                lse = jnp.where(some, m_sc[hr] * C + jnp.log2(safe), LOW)
                hi = lse.astype(jnp.bfloat16).astype(jnp.float32)
                mid = (lse - hi).astype(jnp.bfloat16).astype(jnp.float32)
                lo = lse - hi - mid
                for i, x in enumerate((hi, mid, lo)):
                    stats = jnp.where(lane == h * 8 + i, x, stats)
                for i in range(4):

                    @pl.when(qi == i)
                    def _():
                        outs[i][:T, h * E : (h + 1) * E] = o.astype(jnp.bfloat16)

            flat = stats.T[:ST].astype(jnp.bfloat16)
            for i in range(4):

                @pl.when(qi == i)
                def _():
                    outs[i][T:, :T] = flat
                    outs[i][T:, T:] = jnp.zeros((ST, 2 * E - T), jnp.bfloat16)

        return 0

    lax.fori_loop(0, 4, shard, 0)
    if not last:
        cps = []
        for i, (src, dst) in enumerate(((m_sc, m_out), (l_sc, l_out), (a_sc, a_out))):
            cp = pltpu.make_async_copy(src, dst, ssem.at[i])
            cp.start()
            cps.append(cp)
        for cp in cps:
            cp.wait()


def _flash(first, last, offs, live, ids, qids, qs, blocks, state=()):
    nb = len(blocks)
    rows = 8 * T
    keys = nb * (T + CB)
    if last:
        out_shape = [jax.ShapeDtypeStruct((T + ST, 2 * E), jnp.bfloat16)] * 4
        out_specs = [pl.BlockSpec(memory_space=pltpu.VMEM)] * 4
    else:
        out_shape = [
            jax.ShapeDtypeStruct((rows, 128), jnp.float32),
            jax.ShapeDtypeStruct((rows, 128), jnp.float32),
            jax.ShapeDtypeStruct((rows, E), jnp.float32),
        ]
        out_specs = [pl.BlockSpec(memory_space=pl.ANY)] * 3
    n_in = 4 + nb + len(state)
    return pl.pallas_call(
        functools.partial(_flash_body, nb, first, last),
        out_shape=out_shape,
        grid_spec=pltpu.PrefetchScalarGridSpec(
            num_scalar_prefetch=4,
            grid=(1,),
            in_specs=[pl.BlockSpec(memory_space=pl.ANY)] * n_in,
            out_specs=out_specs,
            scratch_shapes=[
                pltpu.VMEM((4, T, 2 * E), jnp.bfloat16),
                pltpu.VMEM((keys, E), jnp.bfloat16),
                pltpu.VMEM((keys, E), jnp.bfloat16),
                pltpu.VMEM((rows, 128), jnp.float32),
                pltpu.VMEM((rows, 128), jnp.float32),
                pltpu.VMEM((rows, E), jnp.float32),
                pltpu.SemaphoreType.DMA((4,)),
                pltpu.SemaphoreType.DMA((3 * nb,)),
                pltpu.SemaphoreType.DMA((3 * nb,)),
                pltpu.SemaphoreType.DMA((3,)),
            ],
        ),
        compiler_params=pltpu.CompilerParams(vmem_limit_bytes=40 << 20),
        cost_estimate=pl.CostEstimate(
            flops=8 * T * keys * E * 4 * 6 // 10,
            bytes_accessed=keys * E * 4 + rows * E * 6,
            transcendentals=8 * T * keys * 6 // 10,
        ),
    )(offs, live, ids, qids, *qs, *blocks, *state)


def _merge_body(*refs):
    parts, (top, bottom) = refs[:4], refs[4:]
    lses = []
    for p in parts:
        flat = p[T:, :T].astype(jnp.float32)
        lses.append(jnp.concatenate([flat, jnp.zeros((128 - ST, T), jnp.float32)], axis=0).T)
    for h in range(2):
        ls = [s[:, h * 8 : h * 8 + 1] + s[:, h * 8 + 1 : h * 8 + 2] + s[:, h * 8 + 2 : h * 8 + 3] for s in lses]
        peak = functools.reduce(jnp.maximum, ls)
        ws = [jnp.exp2(x - peak) for x in ls]
        inv = 1.0 / functools.reduce(jnp.add, ws)
        o = 0.0
        for p, w in zip(parts, ws):
            o = o + p[:T, h * E : (h + 1) * E].astype(jnp.float32) * (w * inv)
        o = o.astype(jnp.bfloat16)
        top[:, h * E : (h + 1) * E] = o[: T // 2]
        bottom[:, h * E : (h + 1) * E] = o[T // 2 :]


def _merge(parts):
    return pl.pallas_call(
        _merge_body,
        out_shape=[jax.ShapeDtypeStruct((T // 2, 2 * E), jnp.bfloat16)] * 2,
        in_specs=[pl.BlockSpec(memory_space=pltpu.VMEM)] * 4,
        out_specs=[pl.BlockSpec(memory_space=pltpu.VMEM)] * 2,
        cost_estimate=pl.CostEstimate(flops=4 * T * E * 8, bytes_accessed=4 * T * E * 6, transcendentals=T * 16),
    )(*parts)


WP = 64


def _project_body(pos, *refs):
    tops, bots, w_own, pieces = refs[:4], refs[4:8], refs[8], refs[9:17]
    out, wb, ab, wsem, asem = refs[17:]
    cps = [pltpu.make_async_copy(w_own, wb.at[0], wsem.at[0])]
    for i in range(8):
        at = pl.ds(pl.multiple_of(pos[i] * WP, WP), WP)
        for d in range(3):
            cps.append(
                pltpu.make_async_copy(
                    pieces[i].at[pl.ds(d * WP, WP)], wb.at[d + 1, at], wsem.at[1 + 3 * i + d]
                )
            )
    for d in range(4):
        cps.append(pltpu.make_async_copy(tops[d], ab.at[d, pl.ds(0, T // 2)], asem.at[2 * d]))
        cps.append(pltpu.make_async_copy(bots[d], ab.at[d, pl.ds(T // 2, T // 2)], asem.at[2 * d + 1]))
    for cp in cps:
        cp.start()
    for cp in cps:
        cp.wait()
    total = jnp.dot(ab[0], wb[0], preferred_element_type=jnp.float32)
    for d in range(1, 4):
        total = total + jnp.dot(ab[d], wb[d], preferred_element_type=jnp.float32)
    out[...] = total.astype(jnp.bfloat16)


def _project(pos, tops, bots, w_own, pieces):
    cols = w_own.shape[1]
    return pl.pallas_call(
        _project_body,
        out_shape=jax.ShapeDtypeStruct((T, cols), jnp.bfloat16),
        grid_spec=pltpu.PrefetchScalarGridSpec(
            num_scalar_prefetch=1,
            grid=(1,),
            in_specs=[pl.BlockSpec(memory_space=pl.ANY)] * 17,
            out_specs=pl.BlockSpec(memory_space=pltpu.VMEM),
            scratch_shapes=[
                pltpu.VMEM((4, 2 * E, cols), jnp.bfloat16),
                pltpu.VMEM((4, T, 2 * E), jnp.bfloat16),
                pltpu.SemaphoreType.DMA((25,)),
                pltpu.SemaphoreType.DMA((8,)),
            ],
        ),
        compiler_params=pltpu.CompilerParams(vmem_limit_bytes=24 << 20),
        cost_estimate=pl.CostEstimate(flops=2 * T * 8 * E * cols, bytes_accessed=8 * E * cols * 2, transcendentals=0),
    )(pos, *tops, *bots, w_own, *pieces)


def per_device(
    queries,
    span_keys,
    span_values,
    cache_keys,
    cache_values,
    out_weight,
    offsets,
    earlier_block_slot,
    prior_block_count,
):
    me = lax.axis_index("ctx")
    tp = lax.axis_index("tp")
    y, z, x, c = me // (NZ * NX * NC), (me // (NX * NC)) % NZ, (me // NC) % NX, me % NC

    d0 = jnp.concatenate([span_keys, span_values, cache_keys, cache_values], axis=0)
    e0 = _send(d0, dz=1)
    dm = _send(d0, dy=1)
    dp = _send(d0, dy=-1)
    qm = _send(queries, dx=1)
    qp = _send(queries, dx=-1)
    q2 = _send(queries, dx=2)
    em = _send(e0, dy=1)
    ep = _send(e0, dy=-1)
    d2 = _send(dm, dy=1)
    e2 = _send(ep, dy=-1)
    early = [d0, e0, dm, dp]
    late = [em, ep, d2, e2]
    early = early + [_send(b, dc=1) for b in early]
    late = late + [_send(b, dc=1) for b in late]
    steps = [(0, 0), (0, 1), (-1, 0), (1, 0), (-1, 1), (1, 1), (2, 0), (2, 1)]

    def ids_of(part):
        dy = jnp.array([s[0] for s in part] * 2, jnp.int32)
        dz = jnp.array([s[1] for s in part] * 2, jnp.int32)
        dc = jnp.array([0] * len(part) + [1] * len(part), jnp.int32)
        return ((((y + dy + NY) % NY) * NZ + (z + dz) % NZ) * NX + x) * NC + (c + dc) % NC

    dx = jnp.array([0, -1, 1, 2], jnp.int32)
    qids = ((y * NZ + z) * NX + (x + dx + NX) % NX) * NC + c
    slots = jnp.arange(earlier_block_slot.shape[0], dtype=jnp.int32)
    hit = (earlier_block_slot[None, :] == slots[:, None]) & (slots[None, :] < prior_block_count[0])
    live = jnp.sum(hit.astype(jnp.int32), axis=1)

    rows = out_weight.shape[0]
    cols = out_weight.shape[1] // 4
    piece = lax.dynamic_slice_in_dim(out_weight, (x * NC + c) * WP, WP, 0)
    piece, _ = lax.optimization_barrier((piece, e0))
    ws = []
    for d in (1, -1, 2):
        cut = lax.dynamic_slice_in_dim(piece, ((tp + d + 4) % 4) * cols, cols, 1)
        ws.append(_send_tp(cut, d))
    w0 = jnp.concatenate(ws, axis=0)
    w_own = lax.dynamic_slice_in_dim(out_weight, tp * cols, cols, 1)
    pieces = [w0, _send(w0, dx=1), _send(w0, dx=-1), _send(w0, dx=2)]
    pieces = pieces + [_send(w, dc=1) for w in pieces]
    pos = jnp.concatenate(
        [((x + dx + NX) % NX) * NC + c, ((x + dx + NX) % NX) * NC + (c + 1) % NC]
    ).astype(jnp.int32)

    qs = [queries, qm, qp, q2]
    state = _flash(True, False, offsets, live, ids_of(steps[:4]), qids, qs, early)
    parts = _flash(False, True, offsets, live, ids_of(steps[4:]), qids, qs, late, state)
    back = [parts[0], _send(parts[1], dx=-1), _send(parts[2], dx=1), _send(parts[3], dx=2)]
    top, bottom = _merge(back)

    tm, bm = _send_tp(top, 1), _send_tp(bottom, 1)
    tq, bq = _send_tp(top, -1), _send_tp(bottom, -1)
    t2, b2 = _send_tp(tm, 1), _send_tp(bq, -1)
    return _project(pos, [top, tm, tq, t2], [bottom, bm, bq, b2], w_own, pieces)


def solution(mesh):
    placed = (
        P("ctx", "tp"),
        P("ctx", "tp"),
        P("ctx", "tp"),
        P("ctx", "tp"),
        P("ctx", "tp"),
        P("tp", None),
        P(),
        P(),
        P(),
    )
    return jax.shard_map(
        per_device, mesh=mesh, in_specs=placed, out_specs=P("ctx", "tp"), check_vma=False
    )
```

```python
import functools

import numpy as np
import jax
import jax.numpy as jnp
from jax import lax
from jax.experimental import pallas as pl
from jax.experimental.pallas import tpu as pltpu
from jax.sharding import PartitionSpec as P


E = 256
BLK = 64
T = 256
CB = 128
DR = T + CB
NY, NZ, NX, NC = 4, 2, 4, 2
C = np.float32(1.4426950408889634 / 16.0)
LOW = -1e30
OUT = -2e30
TK = 512
UN = 4
H = T // 2
ST = 16


def _ctx(y, z, x, c):
    return (((y % NY) * NZ + z % NZ) * NX + x % NX) * NC + c % NC


def _send(a, dy=0, fz=0, fx=0, fc=0):
    pairs = [
        (_ctx(y, z, x, c), _ctx(y + dy, z ^ fz, x ^ fx, c ^ fc))
        for y in range(NY)
        for z in range(NZ)
        for x in range(NX)
        for c in range(NC)
    ]
    return lax.ppermute(a, "ctx", pairs)


def _swap(a, axis):
    if axis == "tp":
        return lax.all_to_all(a, "tp", 0, 0)
    groups = [
        [_ctx(y, p >> 1, x + (p & 1), c) for p in range(4)]
        for y in range(NY)
        for x in (0, 2)
        for c in range(NC)
    ]
    return lax.all_to_all(a, "ctx", 0, 0, axis_index_groups=groups)


def _send_tp(a, d):
    return lax.ppermute(a, "tp", [(i, (i + d) % 4) for i in range(4)])


def _pack_body(*refs):
    ins, out, sem = refs[:4], refs[4], refs[5]
    cps = []
    for i, r in enumerate(ins):
        at = out.at[pl.ds(i // 2 * T, r.shape[0]), pl.ds(i % 2 * E, E)]
        cps.append(pltpu.make_async_copy(r, at, sem.at[i]))
    for cp in cps:
        cp.start()
    for cp in cps:
        cp.wait()


def _pack(*arrays):
    return pl.pallas_call(
        _pack_body,
        out_shape=jax.ShapeDtypeStruct((DR, 2 * E), jnp.bfloat16),
        in_specs=[pl.BlockSpec(memory_space=pl.ANY)] * 4,
        out_specs=pl.BlockSpec(memory_space=pltpu.VMEM),
        scratch_shapes=[pltpu.SemaphoreType.DMA((4,))],
        compiler_params=pltpu.CompilerParams(vmem_limit_bytes=60 << 20),
    )(*arrays)


def _flash_body(nb, offs, live, ids, qids, *refs):
    nq = 4
    q_in, refs = refs[:nq], refs[nq:]
    blocks, refs = refs[:nb], refs[nb:]
    out, refs = refs[0], refs[1:]
    qb, kv, m_sc, l_sc, a_sc, *rest = refs
    bufs, (pairs, meta, qsem, sem) = rest[:UN], rest[UN:]
    ntile = kv.shape[0] // TK

    copies = []
    for i in range(nq):
        for h in range(2):
            cp = pltpu.make_async_copy(
                q_in[i].at[:, pl.ds(h * E, E)], qb.at[pl.ds((2 * i + h) * T, T)], qsem.at[2 * i + h]
            )
            cp.start()
            copies.append(cp)
    koff = [offs[ids[j]] for j in range(nb)]
    alive = [live[ids[j // 2] * 2 + j % 2] for j in range(2 * nb)]
    n_live = alive[0]
    for a in alive[1:]:
        n_live = n_live + a
    span0 = n_live * BLK
    dead0 = span0 + nb * T
    seen = jnp.int32(0)
    for j in range(nb):
        rank = jnp.int32(0)
        for i in range(nb):
            if i != j:
                rank = rank + (koff[i] < koff[j]).astype(jnp.int32)
        row = pl.multiple_of(span0 + rank * T, BLK)
        cp = pltpu.make_async_copy(
            blocks[j].at[pl.ds(0, T)], kv.at[pl.ds(row, T)], sem.at[3 * j]
        )
        cp.start()
        copies.append(cp)
        for h in range(2):
            on = alive[2 * j + h]
            row = jnp.where(on > 0, seen * BLK, dead0 + (2 * j + h - seen) * BLK)
            row = pl.multiple_of(row, BLK)
            seen = seen + on
            cp = pltpu.make_async_copy(
                blocks[j].at[pl.ds(T + h * BLK, BLK)], kv.at[pl.ds(row, BLK)], sem.at[3 * j + 1 + h]
            )
            cp.start()
            copies.append(cp)

    n = jnp.int32(0)
    lims = []
    for i in range(nq):
        qid = qids[i]
        before = jnp.int32(0)
        own = jnp.int32(0)
        for j in range(nb):
            before = before + (koff[j] < offs[qid]).astype(jnp.int32)
            own = own + (ids[j] == qid).astype(jnp.int32)
        base = span0 + before * T
        meta[0, i] = base
        meta[1, i] = own
        lims.append((base // TK, pl.cdiv(base + own * T, TK)))

    def listed(i, lo, hi, n):
        def put(t, n):
            pairs[0, n] = i
            pairs[1, n] = t
            return n + 1

        return lax.fori_loop(lo, hi, put, n)

    for i in range(nq):
        n = listed(i, jnp.int32(0), jnp.int32(1), n)
    for i in range(nq):
        n = listed(i, jnp.int32(1), lims[i][0], n)
    clear = (n - nq) // UN
    for i in range(nq):
        n = listed(i, jnp.maximum(lims[i][0], 1), lims[i][1], n)
    rest0 = nq + UN * clear
    rest = pl.cdiv(n - rest0, 2)

    def fill(i, _):
        pairs[0, i] = 0
        pairs[1, i] = ntile
        return 0

    lax.fori_loop(n, rest0 + 2 * rest + 1, fill, 0)
    for cp in copies:
        cp.wait()

    def score(i, dst):
        rows = pl.ds(pl.multiple_of(pairs[0, i] * 2 * T, 2 * T), 2 * T)
        keys = pl.ds(pl.multiple_of(jnp.minimum(pairs[1, i], ntile - 1) * TK, TK), TK)
        dst[...] = lax.dot_general(
            qb[rows, :], kv[keys, :E], (((1,), (1,)), ((), ())), preferred_element_type=jnp.float32
        )

    def absorb(i, src, masked, first=False):
        at, t = pairs[0, i], pairs[1, i]
        rows = pl.ds(pl.multiple_of(at * 2 * T, 2 * T), 2 * T)
        keys = pl.ds(pl.multiple_of(jnp.minimum(t, ntile - 1) * TK, TK), TK)
        s = src[...]
        if masked:
            room = meta[0, at] - t * TK
            tok = lax.rem(lax.broadcasted_iota(jnp.int32, (2 * T, 1), 0), T)
            col = lax.broadcasted_iota(jnp.int32, s.shape, 1)
            s = jnp.where(col < room + meta[1, at] * (tok + 1), s, OUT)
        old = jnp.full((2 * T, 128), LOW, jnp.float32) if first else m_sc[rows]
        new = jnp.maximum(old, jnp.max(s, axis=1, keepdims=True))
        p = jnp.exp2((s - jnp.tile(new, (1, TK // 128))) * C)
        part = p[:, :128]
        for j in range(1, TK // 128):
            part = part + p[:, j * 128 : (j + 1) * 128]
        up = jnp.dot(p.astype(jnp.bfloat16), kv[keys, E:], preferred_element_type=jnp.float32)
        if first:
            l_sc[rows] = part
            a_sc[rows] = up
        else:
            f = jnp.exp2((old - new) * C)
            l_sc[rows] = l_sc[rows] * f + part
            a_sc[rows] = a_sc[rows] * jnp.tile(f, (1, 2)) + up
        m_sc[rows] = new

    def tiles(i, count, **how):
        for u in range(count):
            score(i + u + 1, bufs[(u + 1) % count])
            absorb(i + u, bufs[u], **how)
        return 0

    score(0, bufs[0])
    tiles(0, nq, masked=True, first=True)
    lax.fori_loop(0, clear, lambda j, _: tiles(nq + UN * j, UN, masked=False), 0)
    lax.fori_loop(0, rest, lambda j, _: tiles(rest0 + 2 * j, 2, masked=True), 0)

    lane = lax.broadcasted_iota(jnp.int32, (T, 128), 1)
    for i in range(nq):
        to = ((qids[i] >> 1) & 1) + ((qids[i] >> 2) & 2)
        stats = jnp.zeros((T, 128), jnp.float32)
        for h in range(2):
            rows = pl.ds((2 * i + h) * T, T)
            ls = jnp.sum(l_sc[rows], axis=1, keepdims=True)
            some = ls > 0.0
            safe = jnp.where(some, ls, 1.0)
            o = (a_sc[rows] * (1.0 / safe)).astype(jnp.bfloat16)
            lse = jnp.where(some, m_sc[rows] * C + jnp.log2(safe), LOW)
            hi = lse.astype(jnp.bfloat16).astype(jnp.float32)
            mid = (lse - hi).astype(jnp.bfloat16).astype(jnp.float32)
            lo = lse - hi - mid
            for k, x in enumerate((hi, mid, lo)):
                stats = jnp.where(lane == h * 8 + k, x, stats)
            out[to, :T, h * E : (h + 1) * E] = o
        out[to, T:, :T] = stats.T[:ST].astype(jnp.bfloat16)
        out[to, T:, T:] = jnp.zeros((ST, 2 * E - T), jnp.bfloat16)


def _flash(offs, live, ids, qids, qs, blocks):
    nb, nq = len(blocks), len(qs)
    rows = nq * 2 * T
    keys = nb * (T + CB)
    return pl.pallas_call(
        functools.partial(_flash_body, nb),
        out_shape=jax.ShapeDtypeStruct((nq, T + ST, 2 * E), jnp.bfloat16),
        grid_spec=pltpu.PrefetchScalarGridSpec(
            num_scalar_prefetch=4,
            grid=(1,),
            in_specs=[pl.BlockSpec(memory_space=pltpu.HBM)] * (nq + nb),
            out_specs=pl.BlockSpec(memory_space=pltpu.VMEM),
            scratch_shapes=[
                pltpu.VMEM((rows, E), jnp.bfloat16),
                pltpu.VMEM((keys, 2 * E), jnp.bfloat16),
                pltpu.VMEM((rows, 128), jnp.float32),
                pltpu.VMEM((rows, 128), jnp.float32),
                pltpu.VMEM((rows, E), jnp.float32),
                *[pltpu.VMEM((2 * T, TK), jnp.float32)] * UN,
                pltpu.SMEM((2, 128), jnp.int32),
                pltpu.SMEM((2, 8), jnp.int32),
                pltpu.SemaphoreType.DMA((2 * nq,)),
                pltpu.SemaphoreType.DMA((3 * nb,)),
            ],
        ),
        compiler_params=pltpu.CompilerParams(vmem_limit_bytes=60 << 20),
        cost_estimate=pl.CostEstimate(
            flops=rows * keys * E * 4 * 6 // 10,
            bytes_accessed=keys * E * 4 + rows * E * 6,
            transcendentals=rows * keys * 6 // 10,
        ),
    )(offs, live, ids, qids, *qs, *blocks)


def _merge_body(parts, top, bottom):
    lses = []
    for i in range(4):
        flat = parts[i, T:, :T].astype(jnp.float32)
        lses.append(jnp.concatenate([flat, jnp.zeros((128 - ST, T), jnp.float32)], axis=0).T)
    for h in range(2):
        k = h * 8
        ls = [s[:, k : k + 1] + s[:, k + 1 : k + 2] + s[:, k + 2 : k + 3] for s in lses]
        peak = functools.reduce(jnp.maximum, ls)
        ws = [jnp.exp2(x - peak) for x in ls]
        inv = 1.0 / functools.reduce(jnp.add, ws)
        o = 0.0
        for i, w in enumerate(ws):
            o = o + parts[i, :T, h * E : (h + 1) * E].astype(jnp.float32) * (w * inv)
        o = o.astype(jnp.bfloat16)
        top[:, h * E : (h + 1) * E] = o[:H]
        bottom[:, h * E : (h + 1) * E] = o[H:]


def _merge(parts):
    return pl.pallas_call(
        _merge_body,
        out_shape=[jax.ShapeDtypeStruct((H, 2 * E), jnp.bfloat16)] * 2,
        in_specs=[pl.BlockSpec(memory_space=pltpu.VMEM)],
        out_specs=[pl.BlockSpec(memory_space=pltpu.VMEM)] * 2,
        compiler_params=pltpu.CompilerParams(vmem_limit_bytes=6 << 20),
        cost_estimate=pl.CostEstimate(
            flops=4 * T * E * 8, bytes_accessed=4 * T * E * 6, transcendentals=T * 16
        ),
    )(parts)


def _weave_body(n, pos, *refs):
    pieces, outs, sem = refs[:n], refs[n : n + 3], refs[n + 3]
    cps = []
    for i in range(n):
        rows = pieces[i].shape[1]
        at = pl.ds(pl.multiple_of(pos[i], rows), rows)
        for d in range(3):
            cps.append(pltpu.make_async_copy(pieces[i].at[d], outs[d].at[at], sem.at[3 * i + d]))
    for cp in cps:
        cp.start()
    for cp in cps:
        cp.wait()


def _weave(pos, pieces):
    n, (_, rows, width) = len(pieces), pieces[0].shape
    return pl.pallas_call(
        functools.partial(_weave_body, n),
        out_shape=[jax.ShapeDtypeStruct((n * rows, width), jnp.bfloat16)] * 3,
        grid_spec=pltpu.PrefetchScalarGridSpec(
            num_scalar_prefetch=1,
            grid=(1,),
            in_specs=[pl.BlockSpec(memory_space=pltpu.HBM)] * n,
            out_specs=[pl.BlockSpec(memory_space=pltpu.VMEM)] * 3,
            scratch_shapes=[pltpu.SemaphoreType.DMA((3 * n,))],
        ),
        compiler_params=pltpu.CompilerParams(vmem_limit_bytes=12 << 20),
    )(pos, *pieces)


def _project(ws, xs, acc, last):
    n, cols = len(ws), ws[0].shape[1]
    flat = [h for x in xs for h in x]

    def body(*refs):
        wr, xr, rest = refs[:n], list(refs[n : n + len(flat)]), refs[n + len(flat) :]
        out = rest[-1]
        for g in range(2):
            at = slice(g * H, (g + 1) * H)
            k, total = 0, None if acc is None else rest[0][at, :]
            for w, x in zip(wr, xs):
                rows = xr[k][at, :] if len(x) == 1 else xr[k + g][...]
                k += len(x)
                y = jnp.dot(rows, w[...], preferred_element_type=jnp.float32)
                total = y if total is None else total + y
            out[at, :] = total.astype(out.dtype)

    args = list(ws) + flat + ([] if acc is None else [acc])
    return pl.pallas_call(
        body,
        out_shape=jax.ShapeDtypeStruct((T, cols), jnp.bfloat16 if last else jnp.float32),
        in_specs=[pl.BlockSpec(memory_space=pltpu.VMEM)] * len(args),
        out_specs=pl.BlockSpec(memory_space=pltpu.VMEM),
        compiler_params=pltpu.CompilerParams(vmem_limit_bytes=12 << 20),
        cost_estimate=pl.CostEstimate(
            flops=n * 2 * T * 2 * E * cols,
            bytes_accessed=n * 4 * E * cols + 8 * T * cols,
            transcendentals=0,
        ),
    )(*args)


def _tables(me, earlier_block_slot, prior_block_count):
    y, z, x, c = me >> 4, (me >> 3) & 1, (me >> 1) & 3, me & 1
    steps = [(0, 0), (0, 3), (-1, 0), (1, 0), (-1, 3), (1, 3), (2, 0), (2, 3)]
    flip = [(dy, fx, fc) for fc in (0, 1) for dy, fx in steps]
    dy, fx, fc = (jnp.array(a, jnp.int32) for a in zip(*flip))
    ids = (((y + dy) & 3) << 4) + (z << 3) + ((x ^ fx) << 1) + (c ^ fc)
    qids = me ^ jnp.array([0, 2, 8, 10], jnp.int32)
    slots = jnp.arange(earlier_block_slot.shape[0], dtype=jnp.int32)
    hit = (earlier_block_slot[None, :] == slots[:, None]) & (slots[None, :] < prior_block_count[0])
    return ids, qids, jnp.sum(hit.astype(jnp.int32), axis=1)


def per_device(
    queries,
    span_keys,
    span_values,
    cache_keys,
    cache_values,
    out_weight,
    offsets,
    earlier_block_slot,
    prior_block_count,
):
    me = lax.axis_index("ctx")
    tp = lax.axis_index("tp")
    y, c = me >> 4, me & 1

    cols = out_weight.shape[1] // 4
    part = out_weight.shape[0] // 8
    cut = lax.dynamic_slice_in_dim(out_weight, (y * NC + c) * part, part, 0)
    cut = cut.reshape(part, 4, cols).transpose(1, 0, 2)

    d0 = _pack(span_keys, span_values, cache_keys, cache_values)
    e0 = _send(d0, fx=3)
    dm = _send(d0, dy=1)
    dp = _send(d0, dy=-1)
    cd0 = _send(d0, fc=1)
    tables = (*_tables(me, earlier_block_slot, prior_block_count), cut)
    e0, tables = lax.optimization_barrier((e0, tables))
    ids, qids, live, cut = tables
    q3 = _send(queries, fz=1, fx=1)
    q1 = _send(queries, fx=1)
    q2 = _send(queries, fz=1)
    em = _send(e0, dy=1)
    ep = _send(e0, dy=-1)
    ce0 = _send(e0, fc=1)
    d2 = _send(dm, dy=1)
    cdm = _send(dm, fc=1)
    cdp = _send(dp, fc=1)
    e2 = _send(ep, dy=-1)
    cem = _send(em, fc=1)
    cep = _send(ep, fc=1)
    cd2 = _send(d2, fc=1)
    ce2 = _send(e2, fc=1)
    blocks = [d0, e0, dm, dp, em, ep, d2, e2, cd0, ce0, cdm, cdp, cem, cep, cd2, ce2]
    wt = _swap(cut, "tp")
    turn = jnp.array([0, -1, 1, 2], jnp.int32)
    row = ((y + turn) & 3) * (NC * part)
    pos = jnp.concatenate([row + c * part, row + (c ^ 1) * part]).astype(jnp.int32)
    parts = _flash(offsets, live, ids, qids, [queries, q1, q2, q3], blocks)
    wt = jnp.stack([lax.dynamic_index_in_dim(wt, (tp + d) & 3, 0, False) for d in (3, 1, 2)])
    pieces = [wt, _send(wt, dy=1), _send(wt, dy=-1), _send(wt, dy=2)]
    pieces = pieces + [_send(w, fc=1) for w in pieces]
    wm, wp, w2 = _weave(pos, pieces)
    weight, parts = lax.optimization_barrier((out_weight, parts))
    w0 = lax.dynamic_slice_in_dim(weight, tp * cols, cols, 1)

    top, bottom = _merge(_swap(parts, "x"))
    tm, bq = _send_tp(top, 1), _send_tp(bottom, 3)
    tq, bm = _send_tp(top, 3), _send_tp(bottom, 1)
    t2, b2 = _send_tp(tm, 1), _send_tp(bq, 3)
    acc = _project([w0, wm, wp], [[top, bottom], [tm, bm], [tq, bq]], None, False)
    return _project([w2], [[t2, b2]], acc, True)


def solution(mesh):
    placed = (
        P("ctx", "tp"),
        P("ctx", "tp"),
        P("ctx", "tp"),
        P("ctx", "tp"),
        P("ctx", "tp"),
        P("tp", None),
        P(),
        P(),
        P(),
    )

    return jax.shard_map(
        per_device, mesh=mesh, in_specs=placed, out_specs=P("ctx", "tp"), check_vma=False
    )
```

```python
import functools

import numpy as np
import jax
import jax.numpy as jnp
from jax import lax
from jax.experimental import pallas as pl
from jax.experimental.pallas import tpu as pltpu
from jax.sharding import PartitionSpec as P


E = 256
BLK = 64
T = 256
CB = 128
DR = T + CB
NY, NZ, NX, NC = 4, 2, 4, 2
C = np.float32(1.4426950408889634 / 16.0)
LOW = -1e30
OUT = -2e30
TK = 512
UN = 4
H = T // 2
ST = 16


def _ctx(y, z, x, c):
    return (((y % NY) * NZ + z % NZ) * NX + x % NX) * NC + c % NC


def _send(a, dy=0, fz=0, fx=0, fc=0):
    pairs = [
        (_ctx(y, z, x, c), _ctx(y + dy, z ^ fz, x ^ fx, c ^ fc))
        for y in range(NY)
        for z in range(NZ)
        for x in range(NX)
        for c in range(NC)
    ]
    return lax.ppermute(a, "ctx", pairs)


def _swap(a, axis):
    if axis == "tp":
        return lax.all_to_all(a, "tp", 0, 0)
    groups = [
        [_ctx(y, p >> 1, x + (p & 1), c) for p in range(4)]
        for y in range(NY)
        for x in (0, 2)
        for c in range(NC)
    ]
    return lax.all_to_all(a, "ctx", 0, 0, axis_index_groups=groups)


def _send_tp(a, d):
    return lax.ppermute(a, "tp", [(i, (i + d) % 4) for i in range(4)])


def _pack_body(*refs):
    ins, out, sem = refs[:4], refs[4], refs[5]
    cps = []
    for i, r in enumerate(ins):
        at = out.at[pl.ds(i // 2 * T, r.shape[0]), pl.ds(i % 2 * E, E)]
        cps.append(pltpu.make_async_copy(r, at, sem.at[i]))
    for cp in cps:
        cp.start()
    for cp in cps:
        cp.wait()


def _pack(*arrays):
    return pl.pallas_call(
        _pack_body,
        out_shape=jax.ShapeDtypeStruct((DR, 2 * E), jnp.bfloat16),
        in_specs=[pl.BlockSpec(memory_space=pl.ANY)] * 4,
        out_specs=pl.BlockSpec(memory_space=pltpu.VMEM),
        scratch_shapes=[pltpu.SemaphoreType.DMA((4,))],
        compiler_params=pltpu.CompilerParams(vmem_limit_bytes=60 << 20),
    )(*arrays)


def _flash_body(nb, plan, *refs):
    nq = 4
    q_in, refs = refs[:nq], refs[nq:]
    blocks, refs = refs[:nb], refs[nb:]
    out, refs = refs[0], refs[1:]
    qb, kv, m_sc, l_sc, a_sc, *rest = refs
    bufs, (pairs, qsem) = rest[:UN], rest[UN:]
    ntile = kv.shape[0] // TK

    copies = []
    for h in range(2):
        cp = pltpu.make_async_copy(
            q_in[0].at[:, pl.ds(h * E, E)], qb.at[pl.ds(h * T, T)], qsem.at[h]
        )
        cp.start()
        copies.append(cp)
    for i in range(1, nq):
        for h in range(2):
            qb[(2 * i + h) * T : (2 * i + h + 1) * T] = q_in[i][:, h * E : (h + 1) * E]
    for j in range(nb):
        moves = [(0, T, plan[j])]
        moves += [(T + h * BLK, BLK, plan[nb + 2 * j + h]) for h in range(2)]
        for at, size, row in moves:
            kv[pl.ds(pl.multiple_of(row, BLK), size), :] = blocks[j][at : at + size, :]

    n = jnp.int32(0)
    lims = []
    for i in range(nq):
        base, own = plan[3 * nb + i], plan[3 * nb + nq + i]
        lims.append((base // TK, pl.cdiv(base + own * T, TK)))

    def listed(i, lo, hi, n):
        def put(t, n):
            pairs[0, n] = i
            pairs[1, n] = t
            return n + 1

        return lax.fori_loop(lo, hi, put, n)

    for i in range(nq):
        n = listed(i, jnp.int32(0), jnp.int32(1), n)
    for i in range(nq):
        n = listed(i, jnp.int32(1), lims[i][0], n)
    clear = (n - nq) // UN
    for i in range(nq):
        n = listed(i, jnp.maximum(lims[i][0], 1), lims[i][1], n)
    rest0 = nq + UN * clear
    rest = pl.cdiv(n - rest0, 2)

    def fill(i, _):
        pairs[0, i] = 0
        pairs[1, i] = ntile
        return 0

    lax.fori_loop(n, rest0 + 2 * rest + 1, fill, 0)

    def score(i, dst):
        rows = pl.ds(pl.multiple_of(pairs[0, i] * 2 * T, 2 * T), 2 * T)
        keys = pl.ds(pl.multiple_of(jnp.minimum(pairs[1, i], ntile - 1) * TK, TK), TK)
        dst[...] = lax.dot_general(
            qb[rows, :], kv[keys, :E], (((1,), (1,)), ((), ())), preferred_element_type=jnp.float32
        )

    def absorb(i, src, masked, first=False):
        at, t = pairs[0, i], pairs[1, i]
        rows = pl.ds(pl.multiple_of(at * 2 * T, 2 * T), 2 * T)
        keys = pl.ds(pl.multiple_of(jnp.minimum(t, ntile - 1) * TK, TK), TK)
        s = src[...]
        if masked:
            room = plan[3 * nb + at] - t * TK
            tok = lax.rem(lax.broadcasted_iota(jnp.int32, (2 * T, 1), 0), T)
            col = lax.broadcasted_iota(jnp.int32, s.shape, 1)
            s = jnp.where(col < room + plan[3 * nb + nq + at] * (tok + 1), s, OUT)
        old = jnp.full((2 * T, 128), LOW, jnp.float32) if first else m_sc[rows]
        new = jnp.maximum(old, jnp.max(s, axis=1, keepdims=True))
        p = jnp.exp2((s - jnp.tile(new, (1, TK // 128))) * C)
        part = p[:, :128]
        for j in range(1, TK // 128):
            part = part + p[:, j * 128 : (j + 1) * 128]
        up = jnp.dot(p.astype(jnp.bfloat16), kv[keys, E:], preferred_element_type=jnp.float32)
        if first:
            l_sc[rows] = part
            a_sc[rows] = up
        else:
            f = jnp.exp2((old - new) * C)
            l_sc[rows] = l_sc[rows] * f + part
            a_sc[rows] = a_sc[rows] * jnp.tile(f, (1, 2)) + up
        m_sc[rows] = new

    def tiles(i, count, **how):
        for u in range(count):
            score(i + u + 1, bufs[(u + 1) % count])
            absorb(i + u, bufs[u], **how)
        return 0

    for cp in copies:
        cp.wait()
    score(0, bufs[0])
    tiles(0, nq, masked=True, first=True)
    lax.fori_loop(0, clear, lambda j, _: tiles(nq + UN * j, UN, masked=False), 0)
    lax.fori_loop(0, rest, lambda j, _: tiles(rest0 + 2 * j, 2, masked=True), 0)

    lane = lax.broadcasted_iota(jnp.int32, (T, 128), 1)
    for i in range(nq):
        to = plan[3 * nb + 2 * nq + i]
        stats = jnp.zeros((T, 128), jnp.float32)
        for h in range(2):
            rows = pl.ds((2 * i + h) * T, T)
            ls = jnp.sum(l_sc[rows], axis=1, keepdims=True)
            some = ls > 0.0
            safe = jnp.where(some, ls, 1.0)
            o = (a_sc[rows] * (1.0 / safe)).astype(jnp.bfloat16)
            lse = jnp.where(some, m_sc[rows] * C + jnp.log2(safe), LOW)
            hi = lse.astype(jnp.bfloat16).astype(jnp.float32)
            mid = (lse - hi).astype(jnp.bfloat16).astype(jnp.float32)
            lo = lse - hi - mid
            for k, x in enumerate((hi, mid, lo)):
                stats = jnp.where(lane == h * 8 + k, x, stats)
            out[to, :T, h * E : (h + 1) * E] = o
        out[to, T:, :T] = stats.T[:ST].astype(jnp.bfloat16)
        out[to, T:, T:] = jnp.zeros((ST, 2 * E - T), jnp.bfloat16)


def _flash(plan, qs, blocks):
    nb, nq = len(blocks), len(qs)
    rows = nq * 2 * T
    keys = nb * (T + CB)
    return pl.pallas_call(
        functools.partial(_flash_body, nb),
        out_shape=jax.ShapeDtypeStruct((nq, T + ST, 2 * E), jnp.bfloat16),
        grid_spec=pltpu.PrefetchScalarGridSpec(
            num_scalar_prefetch=0,
            grid=(1,),
            in_specs=[
                pl.BlockSpec(memory_space=pltpu.SMEM),
                pl.BlockSpec(memory_space=pl.ANY),
                *[pl.BlockSpec(memory_space=pltpu.VMEM)] * (nq - 1 + nb),
            ],
            out_specs=pl.BlockSpec(memory_space=pltpu.VMEM),
            scratch_shapes=[
                pltpu.VMEM((rows, E), jnp.bfloat16),
                pltpu.VMEM((keys, 2 * E), jnp.bfloat16),
                pltpu.VMEM((rows, 128), jnp.float32),
                pltpu.VMEM((rows, 128), jnp.float32),
                pltpu.VMEM((rows, E), jnp.float32),
                *[pltpu.VMEM((2 * T, TK), jnp.float32)] * UN,
                pltpu.SMEM((2, 128), jnp.int32),
                pltpu.SemaphoreType.DMA((2,)),
            ],
        ),
        compiler_params=pltpu.CompilerParams(vmem_limit_bytes=34 << 20),
        cost_estimate=pl.CostEstimate(
            flops=rows * keys * E * 4 * 6 // 10,
            bytes_accessed=keys * E * 4 + rows * E * 6,
            transcendentals=rows * keys * 6 // 10,
        ),
    )(plan, *qs, *blocks)


def _merge_body(parts, top, bottom):
    lses = []
    for i in range(4):
        flat = parts[i, T:, :T].astype(jnp.float32)
        lses.append(jnp.concatenate([flat, jnp.zeros((128 - ST, T), jnp.float32)], axis=0).T)
    for h in range(2):
        k = h * 8
        ls = [s[:, k : k + 1] + s[:, k + 1 : k + 2] + s[:, k + 2 : k + 3] for s in lses]
        peak = functools.reduce(jnp.maximum, ls)
        ws = [jnp.exp2(x - peak) for x in ls]
        inv = 1.0 / functools.reduce(jnp.add, ws)
        o = 0.0
        for i, w in enumerate(ws):
            o = o + parts[i, :T, h * E : (h + 1) * E].astype(jnp.float32) * (w * inv)
        o = o.astype(jnp.bfloat16)
        top[:, h * E : (h + 1) * E] = o[:H]
        bottom[:, h * E : (h + 1) * E] = o[H:]


def _merge(parts):
    return pl.pallas_call(
        _merge_body,
        out_shape=[jax.ShapeDtypeStruct((H, 2 * E), jnp.bfloat16)] * 2,
        in_specs=[pl.BlockSpec(memory_space=pltpu.VMEM)],
        out_specs=[pl.BlockSpec(memory_space=pltpu.VMEM)] * 2,
        compiler_params=pltpu.CompilerParams(vmem_limit_bytes=6 << 20),
        cost_estimate=pl.CostEstimate(
            flops=4 * T * E * 8, bytes_accessed=4 * T * E * 6, transcendentals=T * 16
        ),
    )(parts)


def _weave_body(n, pos, *refs):
    pieces, outs, sem = refs[:n], refs[n : n + 3], refs[n + 3]
    cps = []
    for i in range(n):
        rows = pieces[i].shape[1]
        at = pl.ds(pl.multiple_of(pos[i], rows), rows)
        for d in range(3):
            cps.append(pltpu.make_async_copy(pieces[i].at[d], outs[d].at[at], sem.at[3 * i + d]))
    for cp in cps:
        cp.start()
    for cp in cps:
        cp.wait()


def _weave(pos, pieces):
    n, (_, rows, width) = len(pieces), pieces[0].shape
    return pl.pallas_call(
        functools.partial(_weave_body, n),
        out_shape=[jax.ShapeDtypeStruct((n * rows, width), jnp.bfloat16)] * 3,
        grid_spec=pltpu.PrefetchScalarGridSpec(
            num_scalar_prefetch=1,
            grid=(1,),
            in_specs=[pl.BlockSpec(memory_space=pltpu.HBM)] * n,
            out_specs=[pl.BlockSpec(memory_space=pltpu.VMEM)] * 3,
            scratch_shapes=[pltpu.SemaphoreType.DMA((3 * n,))],
        ),
        compiler_params=pltpu.CompilerParams(vmem_limit_bytes=12 << 20),
    )(pos, *pieces)


def _project(ws, xs, acc, last):
    n, cols = len(ws), ws[0].shape[1]
    flat = [h for x in xs for h in x]

    def body(*refs):
        wr, xr, rest = refs[:n], list(refs[n : n + len(flat)]), refs[n + len(flat) :]
        out = rest[-1]
        for g in range(2):
            at = slice(g * H, (g + 1) * H)
            k, total = 0, None if acc is None else rest[0][at, :]
            for w, x in zip(wr, xs):
                rows = xr[k][at, :] if len(x) == 1 else xr[k + g][...]
                k += len(x)
                y = jnp.dot(rows, w[...], preferred_element_type=jnp.float32)
                total = y if total is None else total + y
            if last:
                out[:, at] = total.T.astype(out.dtype)
            else:
                out[at, :] = total

    args = list(ws) + flat + ([] if acc is None else [acc])
    return pl.pallas_call(
        body,
        out_shape=jax.ShapeDtypeStruct(*(((cols, T), jnp.bfloat16) if last else ((T, cols), jnp.float32))),
        in_specs=[pl.BlockSpec(memory_space=pltpu.VMEM)] * len(args),
        out_specs=pl.BlockSpec(memory_space=pltpu.VMEM),
        compiler_params=pltpu.CompilerParams(vmem_limit_bytes=12 << 20),
        cost_estimate=pl.CostEstimate(
            flops=n * 2 * T * 2 * E * cols,
            bytes_accessed=n * 4 * E * cols + 8 * T * cols,
            transcendentals=0,
        ),
    )(*args)


STEPS = [(0, 0), (0, 3), (-1, 0), (1, 0), (-1, 3), (1, 3), (2, 0), (2, 3)]


def _plan_body(me, offs, slot_of, count, out, live):
    me = me[0]
    y, z, x, c = me >> 4, (me >> 3) & 1, (me >> 1) & 3, me & 1

    def mark(b, _):
        live[slot_of[b]] = (b < count[0]).astype(jnp.int32)
        return 0

    lax.fori_loop(0, slot_of.shape[0], mark, 0)
    ids = []
    for fc in range(2):
        for dy, fx in STEPS:
            ids.append((((y + dy + NY) & 3) << 4) + (z << 3) + ((x ^ fx) << 1) + (c ^ fc))
    nb = len(ids)
    koff = [offs[i] for i in ids]
    alive = [live[ids[j // 2] * 2 + j % 2] for j in range(2 * nb)]
    n_live = functools.reduce(jnp.add, alive)
    span0 = n_live * BLK
    dead0 = span0 + nb * T
    seen = jnp.int32(0)
    for j in range(nb):
        rank = jnp.int32(0)
        for i in range(nb):
            if i != j:
                rank = rank + (koff[i] < koff[j]).astype(jnp.int32)
        out[j] = span0 + rank * T
        for h in range(2):
            on = alive[2 * j + h]
            out[nb + 2 * j + h] = jnp.where(on > 0, seen * BLK, dead0 + (2 * j + h - seen) * BLK)
            seen = seen + on
    for i, flip in enumerate((0, 2, 8, 10)):
        qid = me ^ flip
        before = jnp.int32(0)
        own = jnp.int32(0)
        for j in range(nb):
            before = before + (koff[j] < offs[qid]).astype(jnp.int32)
            own = own + (ids[j] == qid).astype(jnp.int32)
        out[3 * nb + i] = span0 + before * T
        out[3 * nb + 4 + i] = own
        out[3 * nb + 8 + i] = ((qid >> 1) & 1) + ((qid >> 2) & 2)
    for i in range(3 * nb + 12, out.shape[0]):
        out[i] = jnp.int32(0)


def _plan(me, offsets, earlier_block_slot, prior_block_count):
    return pl.pallas_call(
        _plan_body,
        out_shape=jax.ShapeDtypeStruct((64,), jnp.int32),
        grid_spec=pltpu.PrefetchScalarGridSpec(
            num_scalar_prefetch=4,
            grid=(1,),
            out_specs=pl.BlockSpec(memory_space=pltpu.SMEM),
            scratch_shapes=[pltpu.SMEM(earlier_block_slot.shape, jnp.int32)],
        ),
        compiler_params=pltpu.CompilerParams(vmem_limit_bytes=1 << 20),
    )(me.reshape(1).astype(jnp.int32), offsets, earlier_block_slot, prior_block_count)


def per_device(
    queries,
    span_keys,
    span_values,
    cache_keys,
    cache_values,
    out_weight,
    offsets,
    earlier_block_slot,
    prior_block_count,
):
    me = lax.axis_index("ctx")
    tp = lax.axis_index("tp")
    y, c = me >> 4, me & 1

    cols = out_weight.shape[1] // 4
    part = out_weight.shape[0] // 8
    cut = lax.dynamic_slice_in_dim(out_weight, (y * NC + c) * part, part, 0)
    cut = cut.reshape(part, 4, cols).transpose(1, 0, 2)

    d0 = _pack(span_keys, span_values, cache_keys, cache_values)
    e0 = _send(d0, fx=3)
    dm = _send(d0, dy=1)
    dp = _send(d0, dy=-1)
    cd0 = _send(d0, fc=1)
    tables = (_plan(me, offsets, earlier_block_slot, prior_block_count), cut)
    e0, (plan, cut) = lax.optimization_barrier((e0, tables))
    q3 = _send(queries, fz=1, fx=1)
    q1 = _send(queries, fx=1)
    q2 = _send(queries, fz=1)
    em = _send(e0, dy=1)
    ep = _send(e0, dy=-1)
    ce0 = _send(e0, fc=1)
    d2 = _send(dm, dy=1)
    cdm = _send(dm, fc=1)
    cdp = _send(dp, fc=1)
    e2 = _send(ep, dy=-1)
    cem = _send(em, fc=1)
    cep = _send(ep, fc=1)
    cd2 = _send(d2, fc=1)
    ce2 = _send(e2, fc=1)
    blocks = [d0, e0, dm, dp, em, ep, d2, e2, cd0, ce0, cdm, cdp, cem, cep, cd2, ce2]
    wt = _swap(cut, "tp")
    turn = jnp.array([0, -1, 1, 2], jnp.int32)
    row = ((y + turn) & 3) * (NC * part)
    pos = jnp.concatenate([row + c * part, row + (c ^ 1) * part]).astype(jnp.int32)
    parts = _flash(plan, [queries, q1, q2, q3], blocks)
    wt = jnp.stack([lax.dynamic_index_in_dim(wt, (tp + d) & 3, 0, False) for d in (3, 1, 2)])
    pieces = [wt, _send(wt, dy=1), _send(wt, dy=-1), _send(wt, dy=2)]
    pieces = pieces + [_send(w, fc=1) for w in pieces]
    wm, wp, w2 = _weave(pos, pieces)
    weight, parts = lax.optimization_barrier((out_weight, parts))
    w0 = lax.dynamic_slice_in_dim(weight, tp * cols, cols, 1)

    top, bottom = _merge(_swap(parts, "x"))
    tm, bq = _send_tp(top, 1), _send_tp(bottom, 3)
    tq, bm = _send_tp(top, 3), _send_tp(bottom, 1)
    t2, b2 = _send_tp(tm, 1), _send_tp(bq, 3)
    acc = _project([w0], [[top, bottom]], None, False)
    acc = _project([wm, wp], [[tm, bm], [tq, bq]], acc, False)
    return _project([w2], [[t2, b2]], acc, True).T


def solution(mesh):
    placed = (
        P("ctx", "tp"),
        P("ctx", "tp"),
        P("ctx", "tp"),
        P("ctx", "tp"),
        P("ctx", "tp"),
        P("tp", None),
        P(),
        P(),
        P(),
    )

    return jax.shard_map(
        per_device, mesh=mesh, in_specs=placed, out_specs=P("ctx", "tp"), check_vma=False
    )
```
